768 devices in a mesh: cells: 192 (over y_hi, x, z, core), bands: 4 (over y_lo).
Axes of the slice: x: 4, y: 8 (y_hi: 2, y_lo: 4; y = y_hi * 4 + y_lo), z: 12, core: 2. Of those that a mesh axis runs over, the one named last changes fastest.
Arguments:
- start_bands: bfloat16 [224, 98304], P('bands', 'cells'), may hold values from -24 to 24, as said below
- cell_ham: bfloat16 [192, 729, 729], P('cells'), may hold values from -3 to 4, as said below
- node_index: int32 [192, 729], P('cells'), may hold values from 0 to 98431, as said below
Outputs:
- ortho_bands: bfloat16 [224, 98304], P('bands', 'cells')
The draws below stay inside these ranges and needn't reach their ends.
Inputs may be any that keep to these rules, and one draw needn't show every extreme that they name: `start_bands`: random bands whose scale varies from one partition's nodes to the next and from band to band. `cell_ham`: every cell matrix is symmetric. `node_index`: for a cell of partition p (cells p * 1 to (p + 1) - 1) every entry lies in p * 512 to p * 512 + 639, and each of these 640 indices appears in some cell of partition p.
All inputs are finite; a program needn't handle non-finite values.
Results may differ from the reference program's by a relative error of at most 0.0078.
Values may be sent and summed in bfloat16 or wider, within the bound.
No kernel may reach another device: no remote copies, remote signals or barrier semaphores. Data moves between devices by JAX's collectives and lax.ppermute only.
A program may use at most 64 MiB of HBM per device.

```python
import math
import jax
import jax.numpy as jnp
from jax import lax

CELL_NODES = 729
BANDS = 224
CELL_DEV = 1
NODE_DEV = 512
SHARED = 64
NODE_EXT = 640
CELLS = 192
NODES = 98304
N_CELLS = 192


def draw_start_bands(key, part):
    k_base, k_part, k_band = jax.random.split(jax.random.fold_in(key, 11), 3)
    parts_count = NODES // NODE_DEV
    ramp = jnp.arange(parts_count, dtype=jnp.float32) / (parts_count - 1)
    jitter = jnp.exp(jax.random.uniform(k_part, (parts_count,), jnp.float32, math.log(0.3), 0.0))
    band_scale = jnp.exp(jax.random.uniform(k_band, (BANDS,), jnp.float32, math.log(0.5), math.log(2.0)))
    part_scale = (1.0 + 2.0 * ramp) * jitter
    base = jnp.clip(jax.random.normal(k_base, (BANDS, NODES), jnp.float32), -4.0, 4.0)
    row_scale = jnp.repeat(part_scale, NODE_DEV)
    return (base * band_scale[:, None] * row_scale[None, :]).astype(jnp.bfloat16)


def draw_cell_ham(key, part):
    k_off, k_diag = jax.random.split(jax.random.fold_in(key, 23), 2)
    raw = jnp.clip(jax.random.normal(k_off, (CELLS, CELL_NODES, CELL_NODES), jnp.float32), -4.0, 4.0)
    sym = (raw + jnp.swapaxes(raw, 1, 2)) / math.sqrt(2.0 * CELL_NODES)
    diag = jax.random.uniform(k_diag, (CELLS, CELL_NODES), jnp.float32, 0.5, 2.5)
    eye = jnp.eye(CELL_NODES, dtype=jnp.float32)
    return (sym + diag[:, :, None] * eye[None, :, :]).astype(jnp.bfloat16)


def draw_node_index(key, part):
    parts_count = CELLS // CELL_DEV
    slots = CELL_DEV * CELL_NODES

    def one_part(part_key, position):
        k_extra, k_perm = jax.random.split(part_key, 2)
        extra = jax.random.randint(k_extra, (slots - NODE_EXT,), 0, NODE_EXT, dtype=jnp.int32)
        every = jnp.concatenate([jnp.arange(NODE_EXT, dtype=jnp.int32), extra])
        mixed = jax.random.permutation(k_perm, every)
        return (mixed + position * NODE_DEV).astype(jnp.int32).reshape(CELL_DEV, CELL_NODES)
    part_keys = jax.random.split(jax.random.fold_in(key, 37), parts_count)
    result = jax.vmap(one_part)(part_keys, jnp.arange(parts_count, dtype=jnp.int32))
    return result.reshape(CELLS, CELL_NODES).astype(jnp.int32)


def setup_inputs(seed: int = 0) -> dict:
    arg_keys = jax.random.split(jax.random.key(seed), 4)
    start_bands = draw_start_bands(jax.random.fold_in(arg_keys[3], 71), 0)
    cell_ham = draw_cell_ham(jax.random.fold_in(arg_keys[3], 71), 0)
    node_index = draw_node_index(jax.random.fold_in(arg_keys[3], 71), 0)
    return dict(start_bands=start_bands, cell_ham=cell_ham, node_index=node_index)


filter_center = 2.75
filter_half = 2.25

def next_term(applied, current, previous):
    shifted = (applied - filter_center * current.astype(jnp.float32)) / filter_half
    if previous is None:
        return shifted.astype(jnp.bfloat16)
    return (2.0 * shifted - previous.astype(jnp.float32)).astype(jnp.bfloat16)

def apply_operator(bands_now, cell_ham, node_index):
    band_count = bands_now.shape[0]
    padded = jnp.pad(bands_now, ((0, 0), (SHARED, SHARED)))
    blocks = node_index.reshape(N_CELLS, CELL_DEV * CELL_NODES).astype(jnp.int32)
    hams = cell_ham.reshape(N_CELLS, CELL_DEV, CELL_NODES, CELL_NODES)

    def visit(total, inputs):
        index_block, ham_block = inputs
        columns = jnp.take(padded, index_block, axis=1).reshape(band_count, CELL_DEV, CELL_NODES).astype(jnp.float32)
        product = jnp.einsum('bcj,cij->bci', columns, ham_block.astype(jnp.float32))
        return (total.at[:, index_block].add(product.reshape(band_count, -1)), None)
    total = jnp.zeros((band_count, NODES + 2 * SHARED), jnp.float32)
    total, _ = lax.scan(visit, total, (blocks, hams))
    return total[:, SHARED:SHARED + NODES]

def reference(start_bands, cell_ham, node_index):
    first = next_term(apply_operator(start_bands, cell_ham, node_index), start_bands, None)
    second = next_term(apply_operator(first, cell_ham, node_index), first, start_bands)
    third = next_term(apply_operator(second, cell_ham, node_index), second, first)
    margin = jnp.dot(third.astype(jnp.float32), third.T.astype(jnp.float32), preferred_element_type=jnp.float32) / NODES
    lower = jnp.linalg.cholesky(margin)
    identity = jnp.eye(BANDS, dtype=jnp.float32)
    inverse = lax.linalg.triangular_solve(lower, identity, left_side=True, lower=True)
    return jnp.dot(inverse.astype(jnp.bfloat16).astype(jnp.float32), third.astype(jnp.float32), preferred_element_type=jnp.float32).astype(jnp.bfloat16)
```

```python
import jax
import jax.numpy as jnp
from jax import lax
from jax.sharding import Mesh, PartitionSpec as P

CELL_NODES = 729
BANDS = 224
BLOCK = 56
NODE_DEV = 512
SHARED = 64
NODE_EXT = 640
EDGE = 2 * SHARED
CELLS = ("yh", "x", "z", "core")
INNER = ("z", "core")
OUTER = ("yh", "x", "bands")
N_CELLS = 192
N_INNER = 24
N_OUTER = 32
ROWS = 4
UP = [(i, i + 1) for i in range(N_CELLS - 1)]
DOWN = [(j, i) for i, j in UP]

filter_center = 2.75
filter_half = 2.25


def exchange(to_right, to_left):
    from_left = lax.ppermute(to_right, CELLS, UP)
    from_right = lax.ppermute(to_left, CELLS, DOWN)
    return from_left, from_right


def from_everyone(shard, axis, size):
    copies = jnp.broadcast_to(shard, (size, *shard.shape))
    return lax.all_to_all(copies, axis, split_axis=0, concat_axis=0, tiled=True)


def split(value):
    high = lax.reduce_precision(value, 8, 7)
    return high.astype(jnp.bfloat16), (value - high).astype(jnp.bfloat16)


def dot(a, b, dims):
    return lax.dot_general(a, b, (dims, ((), ())), preferred_element_type=jnp.float32)


def assembled(cell_ham, local_index):
    nodes = lax.broadcasted_iota(jnp.int32, (CELL_NODES, NODE_EXT), 1)
    pick = (local_index[:, None] == nodes).astype(jnp.bfloat16)
    high, low = split(dot(cell_ham, pick, ((1,), (0,))))
    total = dot(pick, high, ((0,), (0,))) + dot(pick, low, ((0,), (0,)))
    return split(total)


def next_term(applied, current, previous):
    shifted = (applied - filter_center * current.astype(jnp.float32)) / filter_half
    if previous is None:
        return shifted.astype(jnp.bfloat16)
    return (2.0 * shifted - previous.astype(jnp.float32)).astype(jnp.bfloat16)


def packed_gram(gathered, third, band):
    full = dot(gathered, third, ((1,), (1,))).reshape(4, BLOCK, BLOCK)
    here = lax.dynamic_index_in_dim(full, band, 0, False)
    one = lax.dynamic_index_in_dim(full, (band + 1) % 4, 0, False)
    two = lax.dynamic_index_in_dim(full, (band + 2) % 4, 0, False)
    half = BLOCK // 2
    top = jnp.concatenate([here, one], axis=1)
    bottom = jnp.concatenate([two[:half], two[half:]], axis=1)
    rows = jnp.concatenate([top, bottom], axis=0)
    rows = jnp.pad(rows, ((0, N_INNER * ROWS - rows.shape[0]), (0, 128 - rows.shape[1])))
    return rows.reshape(N_INNER, ROWS, 128)


def unpacked_gram(rows):
    half = BLOCK // 2
    blocks = {}
    for b in range(4):
        here = rows[b, :BLOCK, :BLOCK]
        one = rows[b, :BLOCK, BLOCK : 2 * BLOCK]
        low = rows[b, BLOCK : BLOCK + half]
        two = jnp.concatenate([low[:, :BLOCK], low[:, BLOCK : 2 * BLOCK]], axis=0)
        c, d = (b + 1) % 4, (b + 2) % 4
        blocks[b, b] = here
        blocks[c, b] = one
        blocks[b, c] = one.T
        blocks[d, b] = two
    return jnp.concatenate([jnp.concatenate([blocks[i, j] for j in range(4)], axis=1) for i in range(4)], axis=0)


def shards(start_bands, cell_ham, node_index):
    partition = lax.axis_index(CELLS)
    band = lax.axis_index("bands")
    left, right = exchange(start_bands[:, NODE_DEV - SHARED :], start_bands[:, :SHARED])
    local_index = node_index.reshape(-1) - partition * NODE_DEV
    high, low = assembled(cell_ham[0], local_index)
    node = lax.broadcasted_iota(jnp.int32, (1, NODE_EXT), 1) + partition * NODE_DEV
    inside = (node >= SHARED) & (node < SHARED + N_CELLS * NODE_DEV)

    def applied(bands_now):
        partial = dot(bands_now, high, ((1,), (0,))) + dot(bands_now, low, ((1,), (0,)))
        from_left, from_right = exchange(partial[:, NODE_EXT - EDGE :], partial[:, :EDGE])
        zeros = jnp.zeros((BLOCK, NODE_EXT - 2 * EDGE), jnp.float32)
        return jnp.where(inside, partial + jnp.concatenate([from_left, zeros, from_right], axis=1), 0.0)

    start = jnp.concatenate([left, start_bands, right], axis=1)
    first = next_term(applied(start), start, None)
    second = next_term(applied(first), first, start)
    third = next_term(applied(second), second, first)[:, SHARED : SHARED + NODE_DEV]

    gathered = from_everyone(third, "bands", 4).reshape(BANDS, NODE_DEV)
    rows = packed_gram(gathered, third, band)
    rows = lax.all_to_all(rows, INNER, split_axis=0, concat_axis=0, tiled=True).sum(axis=0)
    rows = from_everyone(rows, OUTER, N_OUTER).reshape(8, 4, ROWS, 128).sum(axis=0)
    rows = from_everyone(rows, INNER, N_INNER)
    rows = jnp.swapaxes(rows, 0, 1).reshape(4, N_INNER * ROWS, 128)
    margin = unpacked_gram(rows) / float(NODE_DEV * N_CELLS)

    lower = jnp.linalg.cholesky(margin)
    identity = jnp.eye(BANDS, dtype=jnp.float32)
    inverse = lax.linalg.triangular_solve(lower, identity, left_side=True, lower=True)
    band_rows = lax.dynamic_slice_in_dim(inverse, band * BLOCK, BLOCK, 0).astype(jnp.bfloat16)
    return dot(band_rows, gathered, ((1,), (0,))).astype(jnp.bfloat16)


def solution(mesh):
    inner = Mesh(mesh.devices.reshape(2, 4, 12, 2, 4), ("yh", "x", "z", "core", "bands"))
    return jax.shard_map(
        shards,
        mesh=inner,
        in_specs=(P("bands", CELLS), P(CELLS, None, None), P(CELLS, None)),
        out_specs=P("bands", CELLS),
        check_vma=False,
    )
```

```python
import jax
import jax.numpy as jnp
from jax import lax
from jax.experimental import pallas as pl
from jax.experimental.pallas import tpu as pltpu
from jax.sharding import Mesh, PartitionSpec as P

CELL_NODES = 729
BANDS = 224
BLOCK = 56
NODE_DEV = 512
SHARED = 64
NODE_EXT = 640
EDGE = 2 * SHARED
CELLS = ("yh", "x", "z", "core")
SPREAD = ("yh", "x")
OUTER = ("yh", "x", "bands")
N_CELLS = 192
ROWS = 12
PANEL = 32
SWAPS = [(i, i + 1) for i in range(1, N_CELLS - 1, 2)] + [(i + 1, i) for i in range(1, N_CELLS - 1, 2)]

filter_center = 2.75
filter_half = 2.25


def exchange(to_right, to_left):
    first_cell = lax.axis_index("core") == 0
    outer = lax.ppermute(jnp.where(first_cell, to_left, to_right), CELLS, SWAPS)
    inner = lax.ppermute(jnp.where(first_cell, to_right, to_left), "core", [(0, 1), (1, 0)])
    return jnp.where(first_cell, outer, inner), jnp.where(first_cell, inner, outer)


def from_everyone(shard, axis, size):
    copies = jnp.broadcast_to(shard, (size, *shard.shape))
    return lax.all_to_all(copies, axis, split_axis=0, concat_axis=0, tiled=True)


def split(value):
    high = lax.reduce_precision(value, 8, 7)
    return high.astype(jnp.bfloat16), (value - high).astype(jnp.bfloat16)


def dot(a, b, dims):
    return lax.dot_general(a, b, (dims, ((), ())), preferred_element_type=jnp.float32)


def assembled(cell_ham, local_index):
    nodes = lax.broadcasted_iota(jnp.int32, (CELL_NODES, NODE_EXT), 1)
    pick = (local_index[:, None] == nodes).astype(jnp.bfloat16)
    high, low = split(dot(cell_ham, pick, ((1,), (0,))))
    total = dot(pick, high, ((0,), (0,))) + dot(pick, low, ((0,), (0,)))
    return split(total)


def next_term(applied, current, previous):
    shifted = (applied - filter_center * current.astype(jnp.float32)) / filter_half
    if previous is None:
        return shifted.astype(jnp.bfloat16)
    return (2.0 * shifted - previous.astype(jnp.float32)).astype(jnp.bfloat16)


def packed_gram(gathered, third, band):
    full = dot(gathered, third, ((1,), (1,))).reshape(4, BLOCK, BLOCK)
    here = lax.dynamic_index_in_dim(full, band, 0, False)
    one = lax.dynamic_index_in_dim(full, (band + 1) % 4, 0, False)
    two = lax.dynamic_index_in_dim(full, (band + 2) % 4, 0, False)
    half = BLOCK // 2
    top = jnp.concatenate([here, one], axis=1)
    bottom = jnp.concatenate([two[:half], two[half:]], axis=1)
    rows = jnp.concatenate([top, bottom], axis=0)
    rows = jnp.pad(rows, ((0, 8 * ROWS - rows.shape[0]), (0, 128 - rows.shape[1])))
    return rows.reshape(8, 3, 4, 128)


def unpacked_gram(rows):
    half = BLOCK // 2
    blocks = {}
    for b in range(4):
        here = rows[b, :BLOCK, :BLOCK]
        one = rows[b, :BLOCK, BLOCK : 2 * BLOCK]
        low = rows[b, BLOCK : BLOCK + half]
        two = jnp.concatenate([low[:, :BLOCK], low[:, BLOCK : 2 * BLOCK]], axis=0)
        c, d = (b + 1) % 4, (b + 2) % 4
        blocks[b, b] = here
        blocks[c, b] = one
        blocks[b, c] = one.T
        blocks[d, b] = two
    return jnp.concatenate([jnp.concatenate([blocks[i, j] for j in range(4)], axis=1) for i in range(4)], axis=0)


def exact_dot(a, b, dims):
    return lax.dot_general(a, b, (dims, ((), ())), precision=lax.Precision.HIGHEST, preferred_element_type=jnp.float32)


def inverse_factor_kernel(margin_ref, inverse_ref, left_ref):
    left_ref[...] = margin_ref[...]
    at_row = lax.broadcasted_iota(jnp.int32, (BANDS, BANDS), 0)
    at_column = lax.broadcasted_iota(jnp.int32, (BANDS, BANDS), 1)
    inverse_ref[...] = (at_row == at_column).astype(jnp.float32)
    row = lax.broadcasted_iota(jnp.int32, (PANEL, PANEL), 0)
    diagonal = row == lax.broadcasted_iota(jnp.int32, (PANEL, PANEL), 1)
    for start in range(0, BANDS, PANEL):
        stop = start + PANEL
        both = jnp.concatenate([left_ref[start:stop, start:stop], diagonal.astype(jnp.float32)], axis=1)
        for j in range(PANEL):
            factor = both[:, j : j + 1] * (1.0 / both[j : j + 1, j : j + 1])
            both = both - jnp.where(row[:, :1] > j, factor, 0.0) * both[j : j + 1, :]
        pivots = jnp.sum(jnp.where(diagonal, both[:, :PANEL], 0.0), axis=1, keepdims=True)
        scaled = both[:, PANEL:] * lax.rsqrt(pivots)
        upper = exact_dot(scaled, left_ref[start:stop, :], ((1,), (0,)))
        rows = exact_dot(scaled, inverse_ref[start:stop, :], ((1,), (0,)))
        inverse_ref[start:stop, :] = rows
        if stop < BANDS:
            below = upper[:, stop:]
            left_ref[stop:, :] = left_ref[stop:, :] - exact_dot(below, upper, ((0,), (0,)))
            inverse_ref[stop:, :] = inverse_ref[stop:, :] - exact_dot(below, rows, ((0,), (0,)))


def inverse_factor(margin):
    return pl.pallas_call(
        inverse_factor_kernel,
        out_shape=jax.ShapeDtypeStruct((BANDS, BANDS), jnp.float32),
        in_specs=[pl.BlockSpec(memory_space=pltpu.VMEM)],
        out_specs=pl.BlockSpec(memory_space=pltpu.VMEM),
        scratch_shapes=[pltpu.VMEM((BANDS, BANDS), jnp.float32)],
    )(margin)


def shards(start_bands, cell_ham, node_index):
    partition = lax.axis_index(CELLS)
    band = lax.axis_index("bands")
    left, right = exchange(start_bands[:, NODE_DEV - SHARED :], start_bands[:, :SHARED])
    local_index = node_index.reshape(-1) - partition * NODE_DEV
    high, low = assembled(cell_ham[0], local_index)
    node = lax.broadcasted_iota(jnp.int32, (1, NODE_EXT), 1) + partition * NODE_DEV
    inside = (node >= SHARED) & (node < SHARED + N_CELLS * NODE_DEV)

    def applied(bands_now):
        partial = dot(bands_now, high, ((1,), (0,))) + dot(bands_now, low, ((1,), (0,)))
        from_left, from_right = exchange(partial[:, NODE_EXT - EDGE :], partial[:, :EDGE])
        zeros = jnp.zeros((BLOCK, NODE_EXT - 2 * EDGE), jnp.float32)
        return jnp.where(inside, partial + jnp.concatenate([from_left, zeros, from_right], axis=1), 0.0)

    start = jnp.concatenate([left, start_bands, right], axis=1)
    first = next_term(applied(start), start, None)
    second = next_term(applied(first), first, start)
    third = next_term(applied(second), second, first)[:, SHARED : SHARED + NODE_DEV]

    gathered = from_everyone(third, "bands", 4).reshape(BANDS, NODE_DEV)
    rows = packed_gram(gathered, third, band)
    rows = lax.all_to_all(rows, SPREAD, split_axis=0, concat_axis=0, tiled=True).sum(axis=0)
    rows = from_everyone(rows, "z", 12).sum(axis=0)
    rows = rows + lax.ppermute(rows, "core", [(0, 1), (1, 0)])
    rows = from_everyone(rows, OUTER, 32).reshape(8, 4, ROWS, 128)
    rows = jnp.swapaxes(rows, 0, 1).reshape(4, 8 * ROWS, 128)
    margin = unpacked_gram(rows) / float(NODE_DEV * N_CELLS)

    inverse = inverse_factor(margin)
    band_rows = lax.dynamic_slice_in_dim(inverse, band * BLOCK, BLOCK, 0).astype(jnp.bfloat16)
    return dot(band_rows, gathered, ((1,), (0,))).astype(jnp.bfloat16)


def solution(mesh):
    inner = Mesh(mesh.devices.reshape(2, 4, 12, 2, 4), ("yh", "x", "z", "core", "bands"))
    return jax.shard_map(
        shards,
        mesh=inner,
        in_specs=(P("bands", CELLS), P(CELLS, None, None), P(CELLS, None)),
        out_specs=P("bands", CELLS),
        check_vma=False,
    )
```

```python
import jax
import jax.numpy as jnp
from jax import lax
from jax.experimental import pallas as pl
from jax.experimental.pallas import tpu as pltpu
from jax.sharding import Mesh, PartitionSpec as P

CELL_NODES = 729
BANDS = 224
BLOCK = 56
NODE_DEV = 512
SHARED = 64
NODE_EXT = 640
EDGE = 2 * SHARED
CELLS = ("yh", "x", "z", "core")
SPREAD = ("yh", "x")
OUTER = ("yh", "x", "bands")
N_CELLS = 192
ROWS = 12
GROUP = 14
SWAPS = [(i, i + 1) for i in range(1, N_CELLS - 1, 2)] + [(i + 1, i) for i in range(1, N_CELLS - 1, 2)]

filter_center = 2.75
filter_half = 2.25


def exchange(to_right, to_left):
    first_cell = lax.axis_index("core") == 0
    outer = lax.ppermute(jnp.where(first_cell, to_left, to_right), CELLS, SWAPS)
    inner = lax.ppermute(jnp.where(first_cell, to_right, to_left), "core", [(0, 1), (1, 0)])
    return jnp.where(first_cell, outer, inner), jnp.where(first_cell, inner, outer)


def from_everyone(shard, axis, size):
    copies = jnp.broadcast_to(shard, (size, *shard.shape))
    return lax.all_to_all(copies, axis, split_axis=0, concat_axis=0, tiled=True)


def split(value):
    high = lax.reduce_precision(value, 8, 7)
    return high.astype(jnp.bfloat16), (value - high).astype(jnp.bfloat16)


def dot(a, b, dims):
    return lax.dot_general(a, b, (dims, ((), ())), preferred_element_type=jnp.float32)


def assembled(cell_ham, local_index):
    nodes = lax.broadcasted_iota(jnp.int32, (CELL_NODES, NODE_EXT), 1)
    pick = (local_index[:, None] == nodes).astype(jnp.bfloat16)
    high, low = split(dot(cell_ham, pick, ((1,), (0,))))
    total = dot(pick, high, ((0,), (0,))) + dot(pick, low, ((0,), (0,)))
    return split(total)


def next_term(applied, current, previous):
    shifted = (applied - filter_center * current.astype(jnp.float32)) / filter_half
    if previous is None:
        return shifted.astype(jnp.bfloat16)
    return (2.0 * shifted - previous.astype(jnp.float32)).astype(jnp.bfloat16)


def gram_kernel(band_ref, gathered_ref, packed_ref, rows_ref):
    band = band_ref[0]
    other = lax.rem(band + 1, 4)
    low = lax.rem(band, 2)

    def product(i, j):
        return dot(gathered_ref[i], gathered_ref[j], ((1,), (1,)))

    rows_ref[...] = jnp.zeros_like(rows_ref)
    two = product(low, low + 2)
    half = BLOCK // 2
    rows_ref[:BLOCK, :BLOCK] = product(band, band)
    rows_ref[:BLOCK, BLOCK : 2 * BLOCK] = product(jnp.minimum(band, other), jnp.maximum(band, other))
    rows_ref[BLOCK : BLOCK + half, :BLOCK] = two[:half]
    rows_ref[BLOCK : BLOCK + half, BLOCK : 2 * BLOCK] = two[half:]
    for i in range(8):
        for j in range(3):
            packed_ref[i, j] = rows_ref[pl.ds(12 * i + 4 * j, 4), :]


def packed_gram(band, gathered):
    return pl.pallas_call(
        gram_kernel,
        out_shape=jax.ShapeDtypeStruct((8, 3, 4, 128), jnp.float32),
        in_specs=[pl.BlockSpec(memory_space=pltpu.SMEM), pl.BlockSpec(memory_space=pltpu.VMEM)],
        out_specs=pl.BlockSpec(memory_space=pltpu.VMEM),
        scratch_shapes=[pltpu.VMEM((8 * ROWS, 128), jnp.float32)],
    )(band, gathered)


def exact_dot(a, b, dims):
    return lax.dot_general(a, b, (dims, ((), ())), precision=lax.Precision.HIGHEST, preferred_element_type=jnp.float32)


def finish_kernel(band_ref, rows_ref, gathered_ref, out_ref, packed_ref, left_ref, inverse_ref):
    for i in range(8):
        for b in range(4):
            for j in range(3):
                packed_ref[b, pl.ds(12 * i + 4 * j, 4), :] = rows_ref[4 * i + b, j]
    half = BLOCK // 2
    scale = 1.0 / float(NODE_DEV * N_CELLS)
    left_ref[...] = jnp.zeros_like(left_ref)
    for b in range(4):
        c, s = (b + 1) % 4, b * BLOCK
        left_ref[s : s + BLOCK, s : s + BLOCK] = packed_ref[b, :BLOCK, :BLOCK] * scale
        r, t = min(b, c) * BLOCK, max(b, c) * BLOCK
        left_ref[r : r + BLOCK, t : t + BLOCK] = packed_ref[b, :BLOCK, BLOCK : 2 * BLOCK] * scale
        if b < 2:
            t = s + 2 * BLOCK
            left_ref[s : s + half, t : t + BLOCK] = packed_ref[b, BLOCK : BLOCK + half, :BLOCK] * scale
            left_ref[s + half : s + BLOCK, t : t + BLOCK] = packed_ref[b, BLOCK : BLOCK + half, BLOCK : 2 * BLOCK] * scale

    at_row = lax.broadcasted_iota(jnp.int32, (BANDS, BANDS), 0)
    at_column = lax.broadcasted_iota(jnp.int32, (BANDS, BANDS), 1)
    inverse_ref[...] = (at_row == at_column).astype(jnp.float32)
    row = lax.broadcasted_iota(jnp.int32, (BLOCK, 128), 0)
    column = lax.broadcasted_iota(jnp.int32, (BLOCK, 128), 1)
    unit = (row + BLOCK == column).astype(jnp.float32)

    def spread(value, i):
        return jnp.broadcast_to(value[i : i + 1, :], (BLOCK, 128))

    for start in range(0, BANDS, BLOCK):
        stop = start + BLOCK
        corner = left_ref[start:stop, start:stop]
        both = jnp.concatenate([corner, jnp.zeros((BLOCK, 128 - BLOCK), jnp.float32)], axis=1) + unit
        for j in range(0, BLOCK, GROUP):
            columns = [jnp.broadcast_to(both[:, j + k : j + k + 1], (BLOCK, 128)) for k in range(GROUP)]
            lines = [spread(both, j + k) for k in range(GROUP)]
            for k in range(GROUP):
                reciprocal = 1.0 / spread(columns[k], j + k)
                factor = jnp.where(row > j + k, columns[k], 0.0) * reciprocal
                for m in range(k + 1, GROUP):
                    entry = spread(columns[k], j + m)
                    columns[m] = columns[m] - factor * entry
                    lines[m] = lines[m] - (entry * reciprocal) * lines[k]
                both = both - factor * lines[k]
        pivots = jnp.sum(jnp.where(row == column, both, 0.0), axis=1, keepdims=True)
        scaled = both[:, BLOCK : 2 * BLOCK] * lax.rsqrt(pivots)
        lines = exact_dot(scaled, inverse_ref[start:stop, :], ((1,), (0,)))
        inverse_ref[start:stop, :] = lines
        if stop < BANDS:
            upper = exact_dot(scaled, left_ref[start:stop, :], ((1,), (0,)))
            right = upper[:, stop:]
            left_ref[stop:, :] = left_ref[stop:, :] - exact_dot(right, upper, ((0,), (0,)))
            inverse_ref[stop:, :] = inverse_ref[stop:, :] - exact_dot(right, lines, ((0,), (0,)))

    band_rows = inverse_ref[pl.ds(pl.multiple_of(band_ref[0] * BLOCK, 8), BLOCK), :].astype(jnp.bfloat16)
    out_ref[...] = dot(band_rows, gathered_ref[...], ((1,), (0,))).astype(jnp.bfloat16)


def finished(band, rows, gathered):
    vmem = pl.BlockSpec(memory_space=pltpu.VMEM)
    return pl.pallas_call(
        finish_kernel,
        out_shape=jax.ShapeDtypeStruct((BLOCK, NODE_DEV), jnp.bfloat16),
        in_specs=[pl.BlockSpec(memory_space=pltpu.SMEM), vmem, vmem],
        out_specs=vmem,
        scratch_shapes=[
            pltpu.VMEM((4, 8 * ROWS, 128), jnp.float32),
            pltpu.VMEM((BANDS, BANDS), jnp.float32),
            pltpu.VMEM((BANDS, BANDS), jnp.float32),
        ],
    )(band, rows, gathered)


def shards(start_bands, cell_ham, node_index):
    partition = lax.axis_index(CELLS)
    band = lax.axis_index("bands")
    left, right = exchange(start_bands[:, NODE_DEV - SHARED :], start_bands[:, :SHARED])
    local_index = node_index.reshape(-1) - partition * NODE_DEV
    high, low = assembled(cell_ham[0], local_index)
    node = lax.broadcasted_iota(jnp.int32, (1, NODE_EXT), 1) + partition * NODE_DEV
    inside = (node >= SHARED) & (node < SHARED + N_CELLS * NODE_DEV)

    def applied(bands_now):
        partial = dot(bands_now, high, ((1,), (0,))) + dot(bands_now, low, ((1,), (0,)))
        from_left, from_right = exchange(partial[:, NODE_EXT - EDGE :], partial[:, :EDGE])
        zeros = jnp.zeros((BLOCK, NODE_EXT - 2 * EDGE), jnp.float32)
        return jnp.where(inside, partial + jnp.concatenate([from_left, zeros, from_right], axis=1), 0.0)

    start = jnp.concatenate([left, start_bands, right], axis=1)
    first = next_term(applied(start), start, None)
    second = next_term(applied(first), first, start)
    third = next_term(applied(second), second, first)[:, SHARED : SHARED + NODE_DEV]

    gathered = from_everyone(third, "bands", 4)
    place = jnp.full((1,), band, jnp.int32)
    rows = packed_gram(place, gathered)
    rows = lax.all_to_all(rows, SPREAD, split_axis=0, concat_axis=0, tiled=True).sum(axis=0)
    rows = from_everyone(rows, "z", 12).sum(axis=0)
    rows = rows + lax.ppermute(rows, "core", [(0, 1), (1, 0)])
    rows = from_everyone(rows, OUTER, 32)
    return finished(place, rows, gathered.reshape(BANDS, NODE_DEV))


def solution(mesh):
    inner = Mesh(mesh.devices.reshape(2, 4, 12, 2, 4), ("yh", "x", "z", "core", "bands"))
    return jax.shard_map(
        shards,
        mesh=inner,
        in_specs=(P("bands", CELLS), P(CELLS, None, None), P(CELLS, None)),
        out_specs=P("bands", CELLS),
        check_vma=False,
    )
```

```python
import jax
import jax.numpy as jnp
from jax import lax
from jax.experimental import pallas as pl
from jax.experimental.pallas import tpu as pltpu
from jax.sharding import Mesh, PartitionSpec as P

CELL_NODES = 729
BANDS = 224
BLOCK = 56
NODE_DEV = 512
SHARED = 64
NODE_EXT = 640
EDGE = 2 * SHARED
CELLS = ("yh", "x", "z", "core")
SPREAD = ("yh", "x")
OUTER = ("yh", "x", "bands")
N_CELLS = 192
ROWS = 12
GROUP = 14
SWAPS = [(i, i + 1) for i in range(1, N_CELLS - 1, 2)] + [(i + 1, i) for i in range(1, N_CELLS - 1, 2)]

filter_center = 2.75
filter_half = 2.25


def exchange(to_right, to_left):
    first_cell = lax.axis_index("core") == 0
    outer = lax.ppermute(jnp.where(first_cell, to_left, to_right), CELLS, SWAPS)
    inner = lax.ppermute(jnp.where(first_cell, to_right, to_left), "core", [(0, 1), (1, 0)])
    return jnp.where(first_cell, outer, inner), jnp.where(first_cell, inner, outer)


def from_everyone(shard, axis, size):
    copies = jnp.broadcast_to(shard, (size, *shard.shape))
    return lax.all_to_all(copies, axis, split_axis=0, concat_axis=0, tiled=True)


def split(value):
    high = lax.reduce_precision(value, 8, 7)
    return high.astype(jnp.bfloat16), (value - high).astype(jnp.bfloat16)


def dot(a, b, dims):
    return lax.dot_general(a, b, (dims, ((), ())), preferred_element_type=jnp.float32)


def assembled(cell_ham, local_index):
    nodes = lax.broadcasted_iota(jnp.int32, (CELL_NODES, NODE_EXT), 1)
    pick = (local_index[:, None] == nodes).astype(jnp.bfloat16)
    high, low = split(dot(cell_ham, pick, ((1,), (0,))))
    total = dot(pick, high, ((0,), (0,))) + dot(pick, low, ((0,), (0,)))
    return split(total)


def next_term(applied, current, previous):
    shifted = (applied - filter_center * current.astype(jnp.float32)) / filter_half
    if previous is None:
        return shifted.astype(jnp.bfloat16)
    return (2.0 * shifted - previous.astype(jnp.float32)).astype(jnp.bfloat16)


def packed_gram(band, gathered, third):
    full = dot(gathered, third, ((2,), (1,)))
    here = lax.dynamic_index_in_dim(full, band, 0, False)
    one = lax.dynamic_index_in_dim(full, (band + 1) % 4, 0, False)
    two = lax.dynamic_index_in_dim(full, (band + 2) % 4, 0, False)
    half = BLOCK // 2
    top = jnp.concatenate([here, one], axis=1)
    bottom = jnp.concatenate([two[:half], two[half:]], axis=1)
    rows = jnp.concatenate([top, bottom], axis=0)
    rows = jnp.pad(rows, ((0, 8 * ROWS - rows.shape[0]), (0, 128 - rows.shape[1])))
    return rows.reshape(8, 3, 4, 128)


def exact_dot(a, b, dims):
    return lax.dot_general(a, b, (dims, ((), ())), precision=lax.Precision.HIGHEST, preferred_element_type=jnp.float32)


def finish_kernel(band_ref, rows_ref, gathered_ref, out_ref, packed_ref, left_ref, inverse_ref):
    for i in range(8):
        for b in range(4):
            for j in range(3):
                packed_ref[b, pl.ds(12 * i + 4 * j, 4), :] = rows_ref[4 * i + b, j]
    half = BLOCK // 2
    scale = 1.0 / float(NODE_DEV * N_CELLS)
    left_ref[...] = jnp.zeros_like(left_ref)
    for b in range(4):
        c, s = (b + 1) % 4, b * BLOCK
        left_ref[s : s + BLOCK, s : s + BLOCK] = packed_ref[b, :BLOCK, :BLOCK] * scale
        r, t = min(b, c) * BLOCK, max(b, c) * BLOCK
        one = packed_ref[b, :BLOCK, BLOCK : 2 * BLOCK] * scale
        left_ref[r : r + BLOCK, t : t + BLOCK] = one.T if b < 3 else one
        if b >= 2:
            r = s - 2 * BLOCK
            left_ref[r : r + half, s : s + BLOCK] = packed_ref[b, BLOCK : BLOCK + half, :BLOCK] * scale
            left_ref[r + half : r + BLOCK, s : s + BLOCK] = packed_ref[b, BLOCK : BLOCK + half, BLOCK : 2 * BLOCK] * scale

    at_row = lax.broadcasted_iota(jnp.int32, (BANDS, BANDS), 0)
    at_column = lax.broadcasted_iota(jnp.int32, (BANDS, BANDS), 1)
    inverse_ref[...] = (at_row == at_column).astype(jnp.float32)
    row = lax.broadcasted_iota(jnp.int32, (BLOCK, 128), 0)
    column = lax.broadcasted_iota(jnp.int32, (BLOCK, 128), 1)
    unit = (row + BLOCK == column).astype(jnp.float32)

    def spread(value, i):
        return jnp.broadcast_to(value[i : i + 1, :], (BLOCK, 128))

    for start in range(0, BANDS, BLOCK):
        stop = start + BLOCK
        corner = left_ref[start:stop, start:stop]
        both = jnp.concatenate([corner, jnp.zeros((BLOCK, 128 - BLOCK), jnp.float32)], axis=1) + unit
        for j in range(0, BLOCK, GROUP):
            columns = [jnp.broadcast_to(both[:, j + k : j + k + 1], (BLOCK, 128)) for k in range(GROUP)]
            lines = [spread(both, j + k) for k in range(GROUP)]
            for k in range(GROUP):
                reciprocal = 1.0 / spread(columns[k], j + k)
                factor = jnp.where(row > j + k, columns[k], 0.0) * reciprocal
                for m in range(k + 1, GROUP):
                    entry = spread(columns[k], j + m)
                    columns[m] = columns[m] - factor * entry
                    lines[m] = lines[m] - (entry * reciprocal) * lines[k]
                both = both - factor * lines[k]
        pivots = jnp.sum(jnp.where(row == column, both, 0.0), axis=1, keepdims=True)
        scaled = both[:, BLOCK : 2 * BLOCK] * lax.rsqrt(pivots)
        lines = exact_dot(scaled, inverse_ref[start:stop, :], ((1,), (0,)))
        inverse_ref[start:stop, :] = lines
        if stop < BANDS:
            upper = exact_dot(scaled, left_ref[start:stop, :], ((1,), (0,)))
            right = upper[:, stop:]
            left_ref[stop:, :] = left_ref[stop:, :] - exact_dot(right, upper, ((0,), (0,)))
            inverse_ref[stop:, :] = inverse_ref[stop:, :] - exact_dot(right, lines, ((0,), (0,)))

    band_rows = inverse_ref[pl.ds(pl.multiple_of(band_ref[0] * BLOCK, 8), BLOCK), :].astype(jnp.bfloat16)
    out_ref[...] = dot(band_rows, gathered_ref[...], ((1,), (0,))).astype(jnp.bfloat16)


def finished(band, rows, gathered):
    vmem = pl.BlockSpec(memory_space=pltpu.VMEM)
    return pl.pallas_call(
        finish_kernel,
        out_shape=jax.ShapeDtypeStruct((BLOCK, NODE_DEV), jnp.bfloat16),
        in_specs=[pl.BlockSpec(memory_space=pltpu.SMEM), vmem, vmem],
        out_specs=vmem,
        scratch_shapes=[
            pltpu.VMEM((4, 8 * ROWS, 128), jnp.float32),
            pltpu.VMEM((BANDS, BANDS), jnp.float32),
            pltpu.VMEM((BANDS, BANDS), jnp.float32),
        ],
    )(band, rows, gathered)


def shards(start_bands, cell_ham, node_index):
    partition = lax.axis_index(CELLS)
    band = lax.axis_index("bands")
    left, right = exchange(start_bands[:, NODE_DEV - SHARED :], start_bands[:, :SHARED])
    local_index = node_index.reshape(-1) - partition * NODE_DEV
    high, low = assembled(cell_ham[0], local_index)
    node = lax.broadcasted_iota(jnp.int32, (1, NODE_EXT), 1) + partition * NODE_DEV
    inside = (node >= SHARED) & (node < SHARED + N_CELLS * NODE_DEV)

    def applied(bands_now):
        partial = dot(bands_now, high, ((1,), (0,))) + dot(bands_now, low, ((1,), (0,)))
        from_left, from_right = exchange(partial[:, NODE_EXT - EDGE :], partial[:, :EDGE])
        zeros = jnp.zeros((BLOCK, NODE_EXT - 2 * EDGE), jnp.float32)
        return jnp.where(inside, partial + jnp.concatenate([from_left, zeros, from_right], axis=1), 0.0)

    start = jnp.concatenate([left, start_bands, right], axis=1)
    first = next_term(applied(start), start, None)
    second = next_term(applied(first), first, start)
    third = next_term(applied(second), second, first)[:, SHARED : SHARED + NODE_DEV]

    gathered = from_everyone(third, "bands", 4)
    place = jnp.full((1,), band, jnp.int32)
    rows = packed_gram(band, gathered, third)
    rows = lax.all_to_all(rows, SPREAD, split_axis=0, concat_axis=0, tiled=True).sum(axis=0)
    rows = from_everyone(rows, "z", 12).sum(axis=0)
    rows = rows + lax.ppermute(rows, "core", [(0, 1), (1, 0)])
    rows = from_everyone(rows, OUTER, 32)
    return finished(place, rows, gathered.reshape(BANDS, NODE_DEV))


def solution(mesh):
    inner = Mesh(mesh.devices.reshape(2, 4, 12, 2, 4), ("yh", "x", "z", "core", "bands"))
    return jax.shard_map(
        shards,
        mesh=inner,
        in_specs=(P("bands", CELLS), P(CELLS, None, None), P(CELLS, None)),
        out_specs=P("bands", CELLS),
        check_vma=False,
    )
```

```python
import jax
import jax.numpy as jnp
from jax import lax
from jax.experimental import pallas as pl
from jax.experimental.pallas import tpu as pltpu
from jax.sharding import Mesh, PartitionSpec as P

CELL_NODES = 729
BANDS = 224
BLOCK = 56
NODE_DEV = 512
SHARED = 64
NODE_EXT = 640
EDGE = 2 * SHARED
CELLS = ("yh", "x", "z", "core")
SPREAD = ("yh", "x")
OUTER = ("yh", "x", "bands")
N_CELLS = 192
ROWS = 12
GROUP = 14
SWAPS = [(i, i + 1) for i in range(1, N_CELLS - 1, 2)] + [(i + 1, i) for i in range(1, N_CELLS - 1, 2)]

filter_center = 2.75
filter_half = 2.25


def swap_outer(value):
    return lax.ppermute(value, CELLS, SWAPS)


def swap_inner(value):
    return lax.ppermute(value, "core", [(0, 1), (1, 0)])


def from_everyone(shard, axis, size):
    copies = jnp.broadcast_to(shard, (size, *shard.shape))
    return lax.all_to_all(copies, axis, split_axis=0, concat_axis=0, tiled=True)


def split(value):
    high = lax.reduce_precision(value, 8, 7)
    return high.astype(jnp.bfloat16), (value - high).astype(jnp.bfloat16)


def dot(a, b, dims):
    return lax.dot_general(a, b, (dims, ((), ())), preferred_element_type=jnp.float32)


def assembled(cell_ham, local_index):
    nodes = lax.broadcasted_iota(jnp.int32, (CELL_NODES, NODE_EXT), 1)
    pick = (local_index[:, None] == nodes).astype(jnp.bfloat16)
    high, low = split(dot(cell_ham, pick, ((1,), (0,))))
    total = dot(pick, high, ((0,), (0,))) + dot(pick, low, ((0,), (0,)))
    return total


def raw_term(applied, current, previous):
    shifted = (applied - filter_center * current.astype(jnp.float32)) / filter_half
    if previous is None:
        return shifted
    return 2.0 * shifted - previous.astype(jnp.float32)


def next_term(applied, current, previous):
    return raw_term(applied, current, previous).astype(jnp.bfloat16)


def packed_gram(band, gathered, third):
    full = dot(gathered, third, ((2,), (1,)))
    here = lax.dynamic_index_in_dim(full, band, 0, False)
    one = lax.dynamic_index_in_dim(full, (band + 1) % 4, 0, False)
    two = lax.dynamic_index_in_dim(full, (band + 2) % 4, 0, False)
    half = BLOCK // 2
    top = jnp.concatenate([here, one], axis=1)
    bottom = jnp.concatenate([two[:half], two[half:]], axis=1)
    rows = jnp.concatenate([top, bottom], axis=0)
    rows = jnp.pad(rows, ((0, 8 * ROWS - rows.shape[0]), (0, 128 - rows.shape[1])))
    return rows.reshape(8, 3, 4, 128)


def exact_dot(a, b, dims):
    return lax.dot_general(a, b, (dims, ((), ())), precision=lax.Precision.HIGHEST, preferred_element_type=jnp.float32)


def finish_kernel(band_ref, rows_ref, gathered_ref, out_ref, packed_ref, left_ref, inverse_ref):
    for i in range(8):
        for b in range(4):
            for j in range(3):
                packed_ref[b, pl.ds(12 * i + 4 * j, 4), :] = rows_ref[4 * i + b, j]
    half = BLOCK // 2
    scale = 1.0 / float(NODE_DEV * N_CELLS)
    left_ref[...] = jnp.zeros_like(left_ref)
    for b in range(4):
        c, s = (b + 1) % 4, b * BLOCK
        left_ref[s : s + BLOCK, s : s + BLOCK] = packed_ref[b, :BLOCK, :BLOCK] * scale
        r, t = min(b, c) * BLOCK, max(b, c) * BLOCK
        one = packed_ref[b, :BLOCK, BLOCK : 2 * BLOCK] * scale
        left_ref[r : r + BLOCK, t : t + BLOCK] = one.T if b < 3 else one
        if b >= 2:
            r = s - 2 * BLOCK
            left_ref[r : r + half, s : s + BLOCK] = packed_ref[b, BLOCK : BLOCK + half, :BLOCK] * scale
            left_ref[r + half : r + BLOCK, s : s + BLOCK] = packed_ref[b, BLOCK : BLOCK + half, BLOCK : 2 * BLOCK] * scale

    at_row = lax.broadcasted_iota(jnp.int32, (BANDS, BANDS), 0)
    at_column = lax.broadcasted_iota(jnp.int32, (BANDS, BANDS), 1)
    inverse_ref[...] = (at_row == at_column).astype(jnp.float32)
    row = lax.broadcasted_iota(jnp.int32, (BLOCK, 128), 0)
    column = lax.broadcasted_iota(jnp.int32, (BLOCK, 128), 1)
    unit = (row + BLOCK == column).astype(jnp.float32)

    def spread(value, i):
        return jnp.broadcast_to(value[i : i + 1, :], (BLOCK, 128))

    for start in range(0, BANDS, BLOCK):
        stop = start + BLOCK
        corner = left_ref[start:stop, start:stop]
        both = jnp.concatenate([corner, jnp.zeros((BLOCK, 128 - BLOCK), jnp.float32)], axis=1) + unit
        for j in range(0, BLOCK, GROUP):
            columns = [jnp.broadcast_to(both[:, j + k : j + k + 1], (BLOCK, 128)) for k in range(GROUP)]
            lines = [spread(both, j + k) for k in range(GROUP)]
            for k in range(GROUP):
                reciprocal = 1.0 / spread(columns[k], j + k)
                factor = jnp.where(row > j + k, columns[k], 0.0) * reciprocal
                for m in range(k + 1, GROUP):
                    entry = spread(columns[k], j + m)
                    columns[m] = columns[m] - factor * entry
                    lines[m] = lines[m] - (entry * reciprocal) * lines[k]
                both = both - factor * lines[k]
        pivots = jnp.sum(jnp.where(row == column, both, 0.0), axis=1, keepdims=True)
        scaled = both[:, BLOCK : 2 * BLOCK] * lax.rsqrt(pivots)
        lines = exact_dot(scaled, inverse_ref[start:stop, :], ((1,), (0,)))
        inverse_ref[start:stop, :] = lines
        if stop < BANDS:
            upper = exact_dot(scaled, left_ref[start:stop, :], ((1,), (0,)))
            right = upper[:, stop:]
            left_ref[stop:, :] = left_ref[stop:, :] - exact_dot(right, upper, ((0,), (0,)))
            inverse_ref[stop:, :] = inverse_ref[stop:, :] - exact_dot(right, lines, ((0,), (0,)))

    band_rows = inverse_ref[pl.ds(pl.multiple_of(band_ref[0] * BLOCK, 8), BLOCK), :].astype(jnp.bfloat16)
    out_ref[...] = dot(band_rows, gathered_ref[...], ((1,), (0,))).astype(jnp.bfloat16)


def finished(band, rows, gathered):
    vmem = pl.BlockSpec(memory_space=pltpu.VMEM)
    return pl.pallas_call(
        finish_kernel,
        out_shape=jax.ShapeDtypeStruct((BLOCK, NODE_DEV), jnp.bfloat16),
        in_specs=[pl.BlockSpec(memory_space=pltpu.SMEM), vmem, vmem],
        out_specs=vmem,
        scratch_shapes=[
            pltpu.VMEM((4, 8 * ROWS, 128), jnp.float32),
            pltpu.VMEM((BANDS, BANDS), jnp.float32),
            pltpu.VMEM((BANDS, BANDS), jnp.float32),
        ],
    )(band, rows, gathered)


def shards(start_bands, cell_ham, node_index):
    partition = lax.axis_index(CELLS)
    band = lax.axis_index("bands")
    first_cell = lax.axis_index("core") == 0

    def outer(value, width=EDGE):
        return jnp.where(first_cell, value[:, :width], value[:, value.shape[1] - width :])

    def inner(value, width=EDGE):
        return jnp.where(first_cell, value[:, value.shape[1] - width :], value[:, :width])

    def sides(from_outer, from_inner):
        return jnp.where(first_cell, from_outer, from_inner), jnp.where(first_cell, from_inner, from_outer)

    def received(from_outer, from_inner):
        left, right = sides(from_outer, from_inner)
        middle = jnp.zeros((BLOCK, NODE_EXT - 2 * EDGE), jnp.float32)
        return jnp.concatenate([left, middle, right], axis=1)

    left, right = sides(swap_outer(outer(start_bands, SHARED)), swap_inner(inner(start_bands, SHARED)))
    local_index = node_index.reshape(-1) - partition * NODE_DEV
    total = assembled(cell_ham[0], local_index)
    high, low = split(total)
    outer_high, outer_low = outer(high), outer(low)
    corner = jnp.where(first_cell, total[:EDGE, :EDGE], total[NODE_EXT - EDGE :, NODE_EXT - EDGE :])
    node = lax.broadcasted_iota(jnp.int32, (1, NODE_EXT), 1) + partition * NODE_DEV
    inside = (node >= SHARED) & (node < SHARED + N_CELLS * NODE_DEV)

    def masked(value):
        return jnp.where(inside, value, 0.0)

    def times(value, upper, lower):
        return dot(value, upper, ((1,), (0,))) + dot(value, lower, ((1,), (0,)))

    start = jnp.concatenate([left, start_bands, right], axis=1)
    part = times(start, high, low)
    arrived = swap_outer(jnp.concatenate([outer(part), corner], axis=0))
    edge, their_corner = arrived[:BLOCK], arrived[BLOCK:]
    first = next_term(masked(part + received(edge, swap_inner(inner(part)))), start, None)

    part = times(first, high, low)
    within = swap_inner(inner(part))
    mine = raw_term(masked(part + received(jnp.zeros_like(within), within)), first, start)
    mine_high, mine_low = split(mine)
    corner_high, corner_low = split(corner)
    ahead = times(mine_high, outer_high, outer_low) + dot(outer(mine_low), corner_high, ((1,), (0,)))
    arrived = swap_outer(jnp.concatenate([outer(part), ahead], axis=0))
    edge, theirs = arrived[:BLOCK], arrived[BLOCK:]
    second = next_term(masked(part + received(edge, within)), first, start)
    their_high, their_low = split(their_corner)
    sent_high, sent_low = split(outer(part) * (2.0 / filter_half))
    theirs = theirs + times(sent_high, their_high, their_low) + dot(sent_low, their_high, ((1,), (0,)))
    part = times(second, high, low)
    third = next_term(masked(part + received(theirs, swap_inner(inner(part)))), second, first)
    third = third[:, SHARED : SHARED + NODE_DEV]

    gathered = from_everyone(third, "bands", 4)
    place = jnp.full((1,), band, jnp.int32)
    rows = packed_gram(band, gathered, third)
    rows = lax.all_to_all(rows, SPREAD, split_axis=0, concat_axis=0, tiled=True).sum(axis=0)
    rows = from_everyone(rows, "z", 12).sum(axis=0)
    rows = rows + lax.ppermute(rows, "core", [(0, 1), (1, 0)])
    rows = from_everyone(rows, OUTER, 32)
    return finished(place, rows, gathered.reshape(BANDS, NODE_DEV))


def solution(mesh):
    inner = Mesh(mesh.devices.reshape(2, 4, 12, 2, 4), ("yh", "x", "z", "core", "bands"))
    return jax.shard_map(
        shards,
        mesh=inner,
        in_specs=(P("bands", CELLS), P(CELLS, None, None), P(CELLS, None)),
        out_specs=P("bands", CELLS),
        check_vma=False,
    )
```

```python
import jax
import jax.numpy as jnp
from jax import lax
from jax.experimental import pallas as pl
from jax.experimental.pallas import tpu as pltpu
from jax.sharding import Mesh, PartitionSpec as P

CELL_NODES = 729
BANDS = 224
BLOCK = 56
NODE_DEV = 512
SHARED = 64
NODE_EXT = 640
EDGE = 2 * SHARED
CELLS = ("yh", "x", "z", "core")
SPREAD = ("yh", "x")
OUTER = ("yh", "x", "bands")
N_CELLS = 192
ROWS = 12
GROUP = 14
SWAPS = [(i, i + 1) for i in range(1, N_CELLS - 1, 2)] + [(i + 1, i) for i in range(1, N_CELLS - 1, 2)]

filter_center = 2.75
filter_half = 2.25


def swap_outer(value):
    return lax.ppermute(value, CELLS, SWAPS)


def swap_inner(value):
    return lax.ppermute(value, "core", [(0, 1), (1, 0)])


def from_everyone(shard, axis, size):
    copies = jnp.broadcast_to(shard, (size, *shard.shape))
    return lax.all_to_all(copies, axis, split_axis=0, concat_axis=0, tiled=True)


def split(value):
    high = lax.reduce_precision(value, 8, 7)
    return high.astype(jnp.bfloat16), (value - high).astype(jnp.bfloat16)


def dot(a, b, dims):
    return lax.dot_general(a, b, (dims, ((), ())), preferred_element_type=jnp.float32)


def assembled(cell_ham, local_index):
    nodes = lax.broadcasted_iota(jnp.int32, (CELL_NODES, NODE_EXT), 1)
    pick = (local_index[:, None] == nodes).astype(jnp.bfloat16)
    high, low = split(dot(cell_ham, pick, ((1,), (0,))))
    total = dot(pick, high, ((0,), (0,))) + dot(pick, low, ((0,), (0,)))
    return total


def raw_term(applied, current, previous):
    shifted = (applied - filter_center * current.astype(jnp.float32)) / filter_half
    if previous is None:
        return shifted
    return 2.0 * shifted - previous.astype(jnp.float32)


def next_term(applied, current, previous):
    return raw_term(applied, current, previous).astype(jnp.bfloat16)


def packed_gram(band, gathered, third):
    full = dot(gathered, third, ((2,), (1,)))
    here = lax.dynamic_index_in_dim(full, band, 0, False)
    one = lax.dynamic_index_in_dim(full, (band + 1) % 4, 0, False)
    two = lax.dynamic_index_in_dim(full, (band + 2) % 4, 0, False)
    half = BLOCK // 2
    top = jnp.concatenate([here, one], axis=1)
    bottom = jnp.concatenate([two[:half], two[half:]], axis=1)
    rows = jnp.concatenate([top, bottom], axis=0)
    rows = jnp.pad(rows, ((0, 8 * ROWS - rows.shape[0]), (0, 128 - rows.shape[1])))
    return rows.reshape(8, 3, 4, 128)


def exact_dot(a, b, dims):
    return lax.dot_general(a, b, (dims, ((), ())), precision=lax.Precision.HIGHEST, preferred_element_type=jnp.float32)


def finish_kernel(band_ref, rows_ref, gathered_ref, out_ref, packed_ref, left_ref, inverse_ref):
    for i in range(8):
        for b in range(4):
            for j in range(3):
                packed_ref[b, pl.ds(12 * i + 4 * j, 4), :] = rows_ref[4 * i + b, j]
    half = BLOCK // 2
    scale = 1.0 / float(NODE_DEV * N_CELLS)
    left_ref[...] = jnp.zeros_like(left_ref)
    for b in range(4):
        c, s = (b + 1) % 4, b * BLOCK
        left_ref[s : s + BLOCK, s : s + BLOCK] = packed_ref[b, :BLOCK, :BLOCK] * scale
        r, t = min(b, c) * BLOCK, max(b, c) * BLOCK
        one = packed_ref[b, :BLOCK, BLOCK : 2 * BLOCK] * scale
        left_ref[r : r + BLOCK, t : t + BLOCK] = one.T if b < 3 else one
        if b >= 2:
            r = s - 2 * BLOCK
            left_ref[r : r + half, s : s + BLOCK] = packed_ref[b, BLOCK : BLOCK + half, :BLOCK] * scale
            left_ref[r + half : r + BLOCK, s : s + BLOCK] = packed_ref[b, BLOCK : BLOCK + half, BLOCK : 2 * BLOCK] * scale

    at_row = lax.broadcasted_iota(jnp.int32, (BANDS, BANDS), 0)
    at_column = lax.broadcasted_iota(jnp.int32, (BANDS, BANDS), 1)
    inverse_ref[...] = (at_row == at_column).astype(jnp.float32)
    row = lax.broadcasted_iota(jnp.int32, (BLOCK, 128), 0)
    column = lax.broadcasted_iota(jnp.int32, (BLOCK, 128), 1)
    unit = (row + BLOCK == column).astype(jnp.float32)

    def spread(value, i):
        return jnp.broadcast_to(value[i : i + 1, :], (BLOCK, 128))

    for start in range(0, BANDS, BLOCK):
        stop = start + BLOCK
        corner = left_ref[start:stop, start:stop]
        both = jnp.concatenate([corner, jnp.zeros((BLOCK, 128 - BLOCK), jnp.float32)], axis=1) + unit
        for j in range(0, BLOCK, GROUP):
            columns = [jnp.broadcast_to(both[:, j + k : j + k + 1], (BLOCK, 128)) for k in range(GROUP)]
            lines = [spread(both, j + k) for k in range(GROUP)]
            pivot = spread(columns[0], j)
            for k in range(GROUP):
                reciprocal = 1.0 / pivot
                if k + 1 < GROUP:
                    beside = spread(columns[k], j + k + 1)
                    pivot = spread(columns[k + 1], j + k + 1) - beside * beside * reciprocal
                factor = jnp.where(row > j + k, columns[k], 0.0) * reciprocal
                for m in range(k + 1, GROUP):
                    entry = spread(columns[k], j + m)
                    columns[m] = columns[m] - factor * entry
                    lines[m] = lines[m] - (entry * reciprocal) * lines[k]
                both = both - factor * lines[k]
        pivots = jnp.sum(jnp.where(row == column, both, 0.0), axis=1, keepdims=True)
        scaled = both[:, BLOCK : 2 * BLOCK] * lax.rsqrt(pivots)
        lines = exact_dot(scaled, inverse_ref[start:stop, :], ((1,), (0,)))
        inverse_ref[start:stop, :] = lines
        if stop < BANDS:
            upper = exact_dot(scaled, left_ref[start:stop, :], ((1,), (0,)))
            right = upper[:, stop:]
            left_ref[stop:, :] = left_ref[stop:, :] - exact_dot(right, upper, ((0,), (0,)))
            inverse_ref[stop:, :] = inverse_ref[stop:, :] - exact_dot(right, lines, ((0,), (0,)))

    band_rows = inverse_ref[pl.ds(pl.multiple_of(band_ref[0] * BLOCK, 8), BLOCK), :].astype(jnp.bfloat16)
    out_ref[...] = dot(band_rows, gathered_ref[...], ((1,), (0,))).astype(jnp.bfloat16)


def finished(band, rows, gathered):
    vmem = pl.BlockSpec(memory_space=pltpu.VMEM)
    return pl.pallas_call(
        finish_kernel,
        out_shape=jax.ShapeDtypeStruct((BLOCK, NODE_DEV), jnp.bfloat16),
        in_specs=[pl.BlockSpec(memory_space=pltpu.SMEM), vmem, vmem],
        out_specs=vmem,
        scratch_shapes=[
            pltpu.VMEM((4, 8 * ROWS, 128), jnp.float32),
            pltpu.VMEM((BANDS, BANDS), jnp.float32),
            pltpu.VMEM((BANDS, BANDS), jnp.float32),
        ],
    )(band, rows, gathered)


def shards(start_bands, cell_ham, node_index):
    partition = lax.axis_index(CELLS)
    band = lax.axis_index("bands")
    first_cell = lax.axis_index("core") == 0

    def outer(value, width=EDGE):
        return jnp.where(first_cell, value[:, :width], value[:, value.shape[1] - width :])

    def inner(value, width=EDGE):
        return jnp.where(first_cell, value[:, value.shape[1] - width :], value[:, :width])

    def sides(from_outer, from_inner):
        return jnp.where(first_cell, from_outer, from_inner), jnp.where(first_cell, from_inner, from_outer)

    def received(from_outer, from_inner):
        left, right = sides(from_outer, from_inner)
        middle = jnp.zeros((BLOCK, NODE_EXT - 2 * EDGE), jnp.float32)
        return jnp.concatenate([left, middle, right], axis=1)

    none = jnp.zeros((BLOCK, SHARED), jnp.bfloat16)
    left, right = sides(none, swap_inner(inner(start_bands, SHARED)))
    base = jnp.concatenate([left, start_bands, right], axis=1)
    local_index = node_index.reshape(-1) - partition * NODE_DEV
    total = assembled(cell_ham[0], local_index)
    high, low = split(total)
    outer_high, outer_low = outer(high), outer(low)
    corner = jnp.where(first_cell, total[:EDGE, :EDGE], total[NODE_EXT - EDGE :, NODE_EXT - EDGE :])
    node = lax.broadcasted_iota(jnp.int32, (1, NODE_EXT), 1) + partition * NODE_DEV
    inside = (node >= SHARED) & (node < SHARED + N_CELLS * NODE_DEV)

    def masked(value):
        return jnp.where(inside, value, 0.0)

    def times(value, upper, lower):
        return dot(value, upper, ((1,), (0,))) + dot(value, lower, ((1,), (0,)))

    part = times(base, high, low)
    shared = outer(base)
    arrived = swap_outer(jnp.concatenate([outer(part), shared.astype(jnp.float32), corner], axis=0))
    edge, halo, their_corner = arrived[:BLOCK], arrived[BLOCK : 2 * BLOCK].astype(jnp.bfloat16), arrived[2 * BLOCK :]
    their_high, their_low = split(their_corner)
    edge = edge + times(shared, their_high, their_low)
    part = part + dot(halo, outer_high, ((1,), (1,))) + dot(halo, outer_low, ((1,), (1,)))
    left, right = sides(halo, jnp.zeros_like(halo))
    middle = jnp.zeros((BLOCK, NODE_EXT - 2 * EDGE), jnp.bfloat16)
    start = base + jnp.concatenate([left, middle, right], axis=1)
    first = next_term(masked(part + received(edge, swap_inner(inner(part)))), start, None)

    part = times(first, high, low)
    within = swap_inner(inner(part))
    mine = raw_term(masked(part + received(jnp.zeros_like(within), within)), first, start)
    mine_high, mine_low = split(mine)
    corner_high, corner_low = split(corner)
    ahead = times(mine_high, outer_high, outer_low) + dot(outer(mine_low), corner_high, ((1,), (0,)))
    arrived = swap_outer(jnp.concatenate([outer(part), ahead], axis=0))
    edge, theirs = arrived[:BLOCK], arrived[BLOCK:]
    second = next_term(masked(part + received(edge, within)), first, start)
    sent_high, sent_low = split(outer(part) * (2.0 / filter_half))
    theirs = theirs + times(sent_high, their_high, their_low) + dot(sent_low, their_high, ((1,), (0,)))
    part = times(second, high, low)
    third = next_term(masked(part + received(theirs, swap_inner(inner(part)))), second, first)
    third = third[:, SHARED : SHARED + NODE_DEV]

    gathered = from_everyone(third, "bands", 4)
    place = jnp.full((1,), band, jnp.int32)
    rows = packed_gram(band, gathered, third)
    rows = lax.all_to_all(rows, SPREAD, split_axis=0, concat_axis=0, tiled=True).sum(axis=0)
    rows = from_everyone(rows, "z", 12).sum(axis=0)
    rows = rows + lax.ppermute(rows, "core", [(0, 1), (1, 0)])
    rows = from_everyone(rows, OUTER, 32)
    return finished(place, rows, gathered.reshape(BANDS, NODE_DEV))


def solution(mesh):
    inner = Mesh(mesh.devices.reshape(2, 4, 12, 2, 4), ("yh", "x", "z", "core", "bands"))
    return jax.shard_map(
        shards,
        mesh=inner,
        in_specs=(P("bands", CELLS), P(CELLS, None, None), P(CELLS, None)),
        out_specs=P("bands", CELLS),
        check_vma=False,
    )
```

```python
import jax
import jax.numpy as jnp
from jax import lax
from jax.experimental import pallas as pl
from jax.experimental.pallas import tpu as pltpu
from jax.sharding import Mesh, PartitionSpec as P

CELL_NODES = 729
BANDS = 224
BLOCK = 56
NODE_DEV = 512
SHARED = 64
NODE_EXT = 640
EDGE = 2 * SHARED
CELLS = ("yh", "x", "z", "core")
SPREAD = ("yh", "x")
OUTER = ("yh", "x", "bands")
N_CELLS = 192
ROWS = 12
GROUP = 14
SWAPS = [(i, i + 1) for i in range(1, N_CELLS - 1, 2)] + [(i + 1, i) for i in range(1, N_CELLS - 1, 2)]

filter_center = 2.75
filter_half = 2.25


def swap_outer(value):
    return lax.ppermute(value, CELLS, SWAPS)


def swap_inner(value):
    return lax.ppermute(value, "core", [(0, 1), (1, 0)])


def from_everyone(shard, axis, size):
    copies = jnp.broadcast_to(shard, (size, *shard.shape))
    return lax.all_to_all(copies, axis, split_axis=0, concat_axis=0, tiled=True)


def split(value):
    high = lax.reduce_precision(value, 8, 7)
    return high.astype(jnp.bfloat16), (value - high).astype(jnp.bfloat16)


def dot(a, b, dims):
    return lax.dot_general(a, b, (dims, ((), ())), preferred_element_type=jnp.float32)


def one_hot(local_index):
    nodes = lax.broadcasted_iota(jnp.int32, (CELL_NODES, NODE_EXT), 1)
    return (local_index[:, None] == nodes).astype(jnp.bfloat16)


def raw_term(applied, current, previous):
    shifted = (applied - filter_center * current.astype(jnp.float32)) / filter_half
    if previous is None:
        return shifted
    return 2.0 * shifted - previous.astype(jnp.float32)


def next_term(applied, current, previous):
    return raw_term(applied, current, previous).astype(jnp.bfloat16)


def packed_gram(band, gathered, third):
    full = dot(gathered, third, ((2,), (1,)))
    here = lax.dynamic_index_in_dim(full, band, 0, False)
    one = lax.dynamic_index_in_dim(full, (band + 1) % 4, 0, False)
    two = lax.dynamic_index_in_dim(full, (band + 2) % 4, 0, False)
    half = BLOCK // 2
    top = jnp.concatenate([here, one], axis=1)
    bottom = jnp.concatenate([two[:half], two[half:]], axis=1)
    rows = jnp.concatenate([top, bottom], axis=0)
    rows = jnp.pad(rows, ((0, 8 * ROWS - rows.shape[0]), (0, 128 - rows.shape[1])))
    return rows.reshape(8, 3, 4, 128)


def exact_dot(a, b, dims):
    return lax.dot_general(a, b, (dims, ((), ())), precision=lax.Precision.HIGHEST, preferred_element_type=jnp.float32)


def finish_kernel(band_ref, rows_ref, gathered_ref, out_ref, packed_ref, left_ref, inverse_ref):
    for i in range(8):
        for b in range(4):
            for j in range(3):
                packed_ref[b, pl.ds(12 * i + 4 * j, 4), :] = rows_ref[4 * i + b, j]
    half = BLOCK // 2
    scale = 1.0 / float(NODE_DEV * N_CELLS)
    left_ref[...] = jnp.zeros_like(left_ref)
    for b in range(4):
        c, s = (b + 1) % 4, b * BLOCK
        left_ref[s : s + BLOCK, s : s + BLOCK] = packed_ref[b, :BLOCK, :BLOCK] * scale
        r, t = min(b, c) * BLOCK, max(b, c) * BLOCK
        one = packed_ref[b, :BLOCK, BLOCK : 2 * BLOCK] * scale
        left_ref[r : r + BLOCK, t : t + BLOCK] = one.T if b < 3 else one
        if b >= 2:
            r = s - 2 * BLOCK
            left_ref[r : r + half, s : s + BLOCK] = packed_ref[b, BLOCK : BLOCK + half, :BLOCK] * scale
            left_ref[r + half : r + BLOCK, s : s + BLOCK] = packed_ref[b, BLOCK : BLOCK + half, BLOCK : 2 * BLOCK] * scale

    at_row = lax.broadcasted_iota(jnp.int32, (BANDS, BANDS), 0)
    at_column = lax.broadcasted_iota(jnp.int32, (BANDS, BANDS), 1)
    inverse_ref[...] = (at_row == at_column).astype(jnp.float32)
    row = lax.broadcasted_iota(jnp.int32, (BLOCK, 128), 0)
    column = lax.broadcasted_iota(jnp.int32, (BLOCK, 128), 1)
    unit = (row + BLOCK == column).astype(jnp.float32)

    def spread(value, i):
        return jnp.broadcast_to(value[i : i + 1, :], (BLOCK, 128))

    for start in range(0, BANDS, BLOCK):
        stop = start + BLOCK
        corner = left_ref[start:stop, start:stop]
        both = jnp.concatenate([corner, jnp.zeros((BLOCK, 128 - BLOCK), jnp.float32)], axis=1) + unit
        for j in range(0, BLOCK, GROUP):
            columns = [jnp.broadcast_to(both[:, j + k : j + k + 1], (BLOCK, 128)) for k in range(GROUP)]
            lines = [spread(both, j + k) for k in range(GROUP)]
            pivot = spread(columns[0], j)
            for k in range(GROUP):
                reciprocal = 1.0 / pivot
                if k + 1 < GROUP:
                    beside = spread(columns[k], j + k + 1)
                    pivot = spread(columns[k + 1], j + k + 1) - beside * beside * reciprocal
                factor = jnp.where(row > j + k, columns[k], 0.0) * reciprocal
                for m in range(k + 1, GROUP):
                    entry = spread(columns[k], j + m)
                    columns[m] = columns[m] - factor * entry
                    lines[m] = lines[m] - (entry * reciprocal) * lines[k]
                both = both - factor * lines[k]
        pivots = jnp.sum(jnp.where(row == column, both, 0.0), axis=1, keepdims=True)
        scaled = both[:, BLOCK : 2 * BLOCK] * lax.rsqrt(pivots)
        lines = exact_dot(scaled, inverse_ref[start:stop, :], ((1,), (0,)))
        inverse_ref[start:stop, :] = lines
        if stop < BANDS:
            upper = exact_dot(scaled, left_ref[start:stop, :], ((1,), (0,)))
            right = upper[:, stop:]
            left_ref[stop:, :] = left_ref[stop:, :] - exact_dot(right, upper, ((0,), (0,)))
            inverse_ref[stop:, :] = inverse_ref[stop:, :] - exact_dot(right, lines, ((0,), (0,)))

    band_rows = inverse_ref[pl.ds(pl.multiple_of(band_ref[0] * BLOCK, 8), BLOCK), :].astype(jnp.bfloat16)
    out_ref[...] = dot(band_rows, gathered_ref[...], ((1,), (0,))).astype(jnp.bfloat16)


def finished(band, rows, gathered):
    vmem = pl.BlockSpec(memory_space=pltpu.VMEM)
    return pl.pallas_call(
        finish_kernel,
        out_shape=jax.ShapeDtypeStruct((BLOCK, NODE_DEV), jnp.bfloat16),
        in_specs=[pl.BlockSpec(memory_space=pltpu.SMEM), vmem, vmem],
        out_specs=vmem,
        scratch_shapes=[
            pltpu.VMEM((4, 8 * ROWS, 128), jnp.float32),
            pltpu.VMEM((BANDS, BANDS), jnp.float32),
            pltpu.VMEM((BANDS, BANDS), jnp.float32),
        ],
    )(band, rows, gathered)


def shards(start_bands, cell_ham, node_index):
    partition = lax.axis_index(CELLS)
    band = lax.axis_index("bands")
    first_cell = lax.axis_index("core") == 0

    def outer(value, width=EDGE):
        return jnp.where(first_cell, value[:, :width], value[:, value.shape[1] - width :])

    def inner(value, width=EDGE):
        return jnp.where(first_cell, value[:, value.shape[1] - width :], value[:, :width])

    def sides(from_outer, from_inner):
        return jnp.where(first_cell, from_outer, from_inner), jnp.where(first_cell, from_inner, from_outer)

    def received(from_outer, from_inner):
        left, right = sides(from_outer, from_inner)
        middle = jnp.zeros((BLOCK, NODE_EXT - 2 * EDGE), jnp.float32)
        return jnp.concatenate([left, middle, right], axis=1)

    none = jnp.zeros((BLOCK, SHARED), jnp.bfloat16)
    left, right = sides(none, swap_inner(inner(start_bands, SHARED)))
    base = jnp.concatenate([left, start_bands, right], axis=1)
    local_index = node_index.reshape(-1) - partition * NODE_DEV
    pick = one_hot(local_index)
    half_high, half_low = split(dot(cell_ham[0], pick, ((1,), (0,))))
    picked = outer(pick)
    corner = dot(picked, outer(half_high), ((0,), (0,))) + dot(picked, outer(half_low), ((0,), (0,)))
    node = lax.broadcasted_iota(jnp.int32, (1, NODE_EXT), 1) + partition * NODE_DEV
    inside = (node >= SHARED) & (node < SHARED + N_CELLS * NODE_DEV)

    def masked(value):
        return jnp.where(inside, value, 0.0)

    def times(value, upper, lower):
        return dot(value, upper, ((1,), (0,))) + dot(value, lower, ((1,), (0,)))

    part = times(dot(base, pick, ((1,), (1,))).astype(jnp.bfloat16), half_high, half_low)
    shared = outer(base)
    sent = jnp.concatenate([outer(part), shared.astype(jnp.float32), corner], axis=0)
    sent, pick, half_high, half_low = lax.optimization_barrier((sent, pick, half_high, half_low))
    arrived = swap_outer(sent)
    high, low = split(dot(pick, half_high, ((0,), (0,))) + dot(pick, half_low, ((0,), (0,))))
    outer_high, outer_low = outer(high), outer(low)
    edge, halo, their_corner = arrived[:BLOCK], arrived[BLOCK : 2 * BLOCK].astype(jnp.bfloat16), arrived[2 * BLOCK :]
    their_high, their_low = split(their_corner)
    edge = edge + times(shared, their_high, their_low)
    part = part + dot(halo, outer_high, ((1,), (1,))) + dot(halo, outer_low, ((1,), (1,)))
    left, right = sides(halo, jnp.zeros_like(halo))
    middle = jnp.zeros((BLOCK, NODE_EXT - 2 * EDGE), jnp.bfloat16)
    start = base + jnp.concatenate([left, middle, right], axis=1)
    first = next_term(masked(part + received(edge, swap_inner(inner(part)))), start, None)

    part = times(first, high, low)
    within = swap_inner(inner(part))
    mine = raw_term(masked(part + received(jnp.zeros_like(within), within)), first, start)
    mine_high, mine_low = split(mine)
    corner_high, corner_low = split(corner)
    ahead = times(mine_high, outer_high, outer_low) + dot(outer(mine_low), corner_high, ((1,), (0,)))
    arrived = swap_outer(jnp.concatenate([outer(part), ahead], axis=0))
    edge, theirs = arrived[:BLOCK], arrived[BLOCK:]
    second = next_term(masked(part + received(edge, within)), first, start)
    sent_high, sent_low = split(outer(part) * (2.0 / filter_half))
    theirs = theirs + times(sent_high, their_high, their_low) + dot(sent_low, their_high, ((1,), (0,)))
    part = times(second, high, low)
    third = next_term(masked(part + received(theirs, swap_inner(inner(part)))), second, first)
    third = third[:, SHARED : SHARED + NODE_DEV]

    gathered = from_everyone(third, "bands", 4)
    place = jnp.full((1,), band, jnp.int32)
    rows = packed_gram(band, gathered, third)
    rows = lax.all_to_all(rows, SPREAD, split_axis=0, concat_axis=0, tiled=True).sum(axis=0)
    rows = from_everyone(rows, "z", 12).sum(axis=0)
    rows = rows + lax.ppermute(rows, "core", [(0, 1), (1, 0)])
    rows = from_everyone(rows, OUTER, 32)
    return finished(place, rows, gathered.reshape(BANDS, NODE_DEV))


def solution(mesh):
    inner = Mesh(mesh.devices.reshape(2, 4, 12, 2, 4), ("yh", "x", "z", "core", "bands"))
    return jax.shard_map(
        shards,
        mesh=inner,
        in_specs=(P("bands", CELLS), P(CELLS, None, None), P(CELLS, None)),
        out_specs=P("bands", CELLS),
        check_vma=False,
    )
```

```python
import jax
import jax.numpy as jnp
from jax import lax
from jax.experimental import pallas as pl
from jax.experimental.pallas import tpu as pltpu
from jax.sharding import Mesh, PartitionSpec as P

CELL_NODES = 729
BANDS = 224
BLOCK = 56
NODE_DEV = 512
SHARED = 64
NODE_EXT = 640
EDGE = 2 * SHARED
CELLS = ("yh", "x", "z", "core")
SPREAD = ("yh", "x")
OUTER = ("yh", "x", "bands")
N_CELLS = 192
ROWS = 12
GROUP = 14
SWAPS = [(i, i + 1) for i in range(1, N_CELLS - 1, 2)] + [(i + 1, i) for i in range(1, N_CELLS - 1, 2)]

filter_center = 2.75
filter_half = 2.25


def swap_outer(value):
    return lax.ppermute(value, CELLS, SWAPS)


def swap_inner(value):
    return lax.ppermute(value, "core", [(0, 1), (1, 0)])


def from_everyone(shard, axis, size):
    copies = jnp.broadcast_to(shard, (size, *shard.shape))
    return lax.all_to_all(copies, axis, split_axis=0, concat_axis=0, tiled=True)


def split(value):
    high = lax.reduce_precision(value, 8, 7)
    return high.astype(jnp.bfloat16), (value - high).astype(jnp.bfloat16)


def dot(a, b, dims):
    return lax.dot_general(a, b, (dims, ((), ())), preferred_element_type=jnp.float32)


def one_hot(local_index):
    nodes = lax.broadcasted_iota(jnp.int32, (CELL_NODES, NODE_EXT), 1)
    return (local_index[:, None] == nodes).astype(jnp.bfloat16)


def raw_term(applied, current, previous):
    shifted = (applied - filter_center * current.astype(jnp.float32)) / filter_half
    if previous is None:
        return shifted
    return 2.0 * shifted - previous.astype(jnp.float32)


def next_term(applied, current, previous):
    return raw_term(applied, current, previous).astype(jnp.bfloat16)


def packed_gram(band, gathered, third):
    full = dot(gathered, third, ((2,), (1,)))
    here = lax.dynamic_index_in_dim(full, band, 0, False)
    one = lax.dynamic_index_in_dim(full, (band + 1) % 4, 0, False)
    two = lax.dynamic_index_in_dim(full, (band + 2) % 4, 0, False)
    half = BLOCK // 2
    top = jnp.concatenate([here, one], axis=1)
    bottom = jnp.concatenate([two[:half], two[half:]], axis=1)
    rows = jnp.concatenate([top, bottom], axis=0)
    rows = jnp.pad(rows, ((0, 8 * ROWS - rows.shape[0]), (0, 128 - rows.shape[1])))
    return rows.reshape(8, 3, 4, 128)


def exact_dot(a, b, dims):
    return lax.dot_general(a, b, (dims, ((), ())), precision=lax.Precision.HIGHEST, preferred_element_type=jnp.float32)


def finish_kernel(band_ref, rows_ref, gathered_ref, out_ref, packed_ref, left_ref):
    for i in range(8):
        for b in range(4):
            for j in range(3):
                packed_ref[b, pl.ds(12 * i + 4 * j, 4), :] = rows_ref[4 * i + b, j]
    half = BLOCK // 2
    scale = 1.0 / float(NODE_DEV * N_CELLS)
    left_ref[...] = jnp.zeros_like(left_ref)
    for b in range(4):
        c, s = (b + 1) % 4, b * BLOCK
        left_ref[s : s + BLOCK, s : s + BLOCK] = packed_ref[b, :BLOCK, :BLOCK] * scale
        r, t = min(b, c) * BLOCK, max(b, c) * BLOCK
        one = packed_ref[b, :BLOCK, BLOCK : 2 * BLOCK] * scale
        left_ref[r : r + BLOCK, t : t + BLOCK] = one.T if b < 3 else one
        if b >= 2:
            r = s - 2 * BLOCK
            left_ref[r : r + half, s : s + BLOCK] = packed_ref[b, BLOCK : BLOCK + half, :BLOCK] * scale
            left_ref[r + half : r + BLOCK, s : s + BLOCK] = packed_ref[b, BLOCK : BLOCK + half, BLOCK : 2 * BLOCK] * scale

    row = lax.broadcasted_iota(jnp.int32, (BLOCK, 128), 0)
    column = lax.broadcasted_iota(jnp.int32, (BLOCK, 128), 1)
    unit = (row + BLOCK == column).astype(jnp.float32)

    def spread(value, i):
        return jnp.broadcast_to(value[i : i + 1, :], (BLOCK, 128))

    for start in range(0, BANDS, BLOCK):
        stop = start + BLOCK
        corner = left_ref[start:stop, start:stop]
        both = jnp.concatenate([corner, jnp.zeros((BLOCK, 128 - BLOCK), jnp.float32)], axis=1) + unit
        for j in range(0, BLOCK, GROUP):
            columns = [jnp.broadcast_to(both[:, j + k : j + k + 1], (BLOCK, 128)) for k in range(GROUP)]
            lines = [spread(both, j + k) for k in range(GROUP)]
            pivot = spread(columns[0], j)
            for k in range(GROUP):
                reciprocal = 1.0 / pivot
                if k + 1 < GROUP:
                    beside = spread(columns[k], j + k + 1)
                    pivot = spread(columns[k + 1], j + k + 1) - beside * beside * reciprocal
                factor = jnp.where(row > j + k, columns[k], 0.0) * reciprocal
                for m in range(k + 1, GROUP):
                    entry = spread(columns[k], j + m)
                    columns[m] = columns[m] - factor * entry
                    lines[m] = lines[m] - (entry * reciprocal) * lines[k]
                both = both - factor * lines[k]
        pivots = jnp.sum(jnp.where(row == column, both, 0.0), axis=1, keepdims=True)
        scaled = both[:, BLOCK : 2 * BLOCK] * lax.rsqrt(pivots)
        left_ref[start:stop, start:stop] = unit[:, BLOCK : 2 * BLOCK]
        lines = exact_dot(scaled, left_ref[start:stop, :], ((1,), (0,)))
        left_ref[start:stop, :] = lines
        if stop < BANDS:
            left_ref[stop:, start:stop] = jnp.zeros((BANDS - stop, BLOCK), jnp.float32)
            left_ref[stop:, :] = left_ref[stop:, :] - exact_dot(lines[:, stop:], lines, ((0,), (0,)))

    first_row = band_ref[0] * BLOCK
    band_rows = left_ref[pl.ds(pl.multiple_of(first_row, 8), BLOCK), :]
    passed = lax.broadcasted_iota(jnp.int32, (BLOCK, BANDS), 1) < first_row + BLOCK
    band_rows = jnp.where(passed, band_rows, 0.0).astype(jnp.bfloat16)
    out_ref[...] = dot(band_rows, gathered_ref[...], ((1,), (0,))).astype(jnp.bfloat16)


def finished(band, rows, gathered):
    vmem = pl.BlockSpec(memory_space=pltpu.VMEM)
    return pl.pallas_call(
        finish_kernel,
        out_shape=jax.ShapeDtypeStruct((BLOCK, NODE_DEV), jnp.bfloat16),
        in_specs=[pl.BlockSpec(memory_space=pltpu.SMEM), vmem, vmem],
        out_specs=vmem,
        scratch_shapes=[
            pltpu.VMEM((4, 8 * ROWS, 128), jnp.float32),
            pltpu.VMEM((BANDS, BANDS), jnp.float32),
        ],
    )(band, rows, gathered)


def shards(start_bands, cell_ham, node_index):
    partition = lax.axis_index(CELLS)
    band = lax.axis_index("bands")
    first_cell = lax.axis_index("core") == 0

    def outer(value, width=EDGE):
        return jnp.where(first_cell, value[:, :width], value[:, value.shape[1] - width :])

    def inner(value, width=EDGE):
        return jnp.where(first_cell, value[:, value.shape[1] - width :], value[:, :width])

    def sides(from_outer, from_inner):
        return jnp.where(first_cell, from_outer, from_inner), jnp.where(first_cell, from_inner, from_outer)

    def received(from_outer, from_inner):
        left, right = sides(from_outer, from_inner)
        middle = jnp.zeros((BLOCK, NODE_EXT - 2 * EDGE), jnp.float32)
        return jnp.concatenate([left, middle, right], axis=1)

    none = jnp.zeros((BLOCK, SHARED), jnp.bfloat16)
    left, right = sides(none, swap_inner(inner(start_bands, SHARED)))
    base = jnp.concatenate([left, start_bands, right], axis=1)
    local_index = node_index.reshape(-1) - partition * NODE_DEV
    pick = one_hot(local_index)
    half_high, half_low = split(dot(cell_ham[0], pick, ((1,), (0,))))
    picked = outer(pick)
    corner = dot(picked, outer(half_high), ((0,), (0,))) + dot(picked, outer(half_low), ((0,), (0,)))
    node = lax.broadcasted_iota(jnp.int32, (1, NODE_EXT), 1) + partition * NODE_DEV
    inside = (node >= SHARED) & (node < SHARED + N_CELLS * NODE_DEV)

    def masked(value):
        return jnp.where(inside, value, 0.0)

    def times(value, upper, lower):
        return dot(value, upper, ((1,), (0,))) + dot(value, lower, ((1,), (0,)))

    part = times(dot(base, pick, ((1,), (1,))).astype(jnp.bfloat16), half_high, half_low)
    shared = outer(base)
    sent = jnp.concatenate([outer(part), shared.astype(jnp.float32), corner], axis=0)
    sent, pick, half_high, half_low = lax.optimization_barrier((sent, pick, half_high, half_low))
    arrived = swap_outer(sent)
    high, low = split(dot(pick, half_high, ((0,), (0,))) + dot(pick, half_low, ((0,), (0,))))
    outer_high, outer_low = outer(high), outer(low)
    edge, halo, their_corner = arrived[:BLOCK], arrived[BLOCK : 2 * BLOCK].astype(jnp.bfloat16), arrived[2 * BLOCK :]
    their_high, their_low = split(their_corner)
    edge = edge + times(shared, their_high, their_low)
    part = part + dot(halo, outer_high, ((1,), (1,))) + dot(halo, outer_low, ((1,), (1,)))
    left, right = sides(halo, jnp.zeros_like(halo))
    middle = jnp.zeros((BLOCK, NODE_EXT - 2 * EDGE), jnp.bfloat16)
    start = base + jnp.concatenate([left, middle, right], axis=1)
    first = next_term(masked(part + received(edge, swap_inner(inner(part)))), start, None)

    part = times(first, high, low)
    within = swap_inner(inner(part))
    mine = raw_term(masked(part + received(jnp.zeros_like(within), within)), first, start)
    mine_high, mine_low = split(mine)
    corner_high, corner_low = split(corner)
    ahead = times(mine_high, outer_high, outer_low) + dot(outer(mine_low), corner_high, ((1,), (0,)))
    arrived = swap_outer(jnp.concatenate([outer(part), ahead], axis=0))
    edge, theirs = arrived[:BLOCK], arrived[BLOCK:]
    second = next_term(masked(part + received(edge, within)), first, start)
    sent_high, sent_low = split(outer(part) * (2.0 / filter_half))
    theirs = theirs + times(sent_high, their_high, their_low) + dot(sent_low, their_high, ((1,), (0,)))
    part = times(second, high, low)
    third = next_term(masked(part + received(theirs, swap_inner(inner(part)))), second, first)
    third = third[:, SHARED : SHARED + NODE_DEV]

    gathered = from_everyone(third, "bands", 4)
    place = jnp.full((1,), band, jnp.int32)
    rows = packed_gram(band, gathered, third)
    rows = lax.all_to_all(rows, SPREAD, split_axis=0, concat_axis=0, tiled=True).sum(axis=0)
    rows = from_everyone(rows, "z", 12).sum(axis=0)
    rows = rows + lax.ppermute(rows, "core", [(0, 1), (1, 0)])
    rows = from_everyone(rows, OUTER, 32)
    return finished(place, rows, gathered.reshape(BANDS, NODE_DEV))


def solution(mesh):
    inner = Mesh(mesh.devices.reshape(2, 4, 12, 2, 4), ("yh", "x", "z", "core", "bands"))
    return jax.shard_map(
        shards,
        mesh=inner,
        in_specs=(P("bands", CELLS), P(CELLS, None, None), P(CELLS, None)),
        out_specs=P("bands", CELLS),
        check_vma=False,
    )
```
